256 devices in a mesh: phase: 32 (over z, x_hi, core), gz: 8 (over y, x_lo).
Axes of the slice: x: 4 (x_hi: 2, x_lo: 2; x = x_hi * 2 + x_lo), y: 4, z: 8, core: 2. Of those that a mesh axis runs over, the one named last changes fastest.
Arguments:
- velocity: float32 [32, 3, 512, 16, 128], P('phase', None, 'gz'), may hold values from -3 to 3
- image: float32 [32, 512, 16, 128], P('phase', 'gz'), may hold values from -6 to 6
- target: float32 [32, 512, 16, 128], P('phase', 'gz'), may hold values from -6 to 6
Outputs:
- adjoint: float32 [32, 512, 16, 128], P('phase', 'gz')
- smoothed: float32 [32, 3, 512, 16, 128], P('phase', None, 'gz')
The draws below stay inside these ranges and needn't reach their ends.
All inputs are finite; a program needn't handle non-finite values.
Results may differ from the reference program's by a relative error of at most 0.00002.
Values sent between devices are 32-bit elements; how exact they have to be, the bound alone decides.
A program may use at most 64 MiB of HBM per device.

```python
import jax
import jax.numpy as jnp
from jax import lax

XW = 16
YW = 128
STEPS = 4
TAPS = 4
PHASES = 32
NZ = 512


def level_of(stream_key, shape, split, smallest, largest):
    gain = 1.0
    for position, blocks in split:
        heights = jax.random.uniform(jax.random.fold_in(jax.random.fold_in(stream_key, 6), position), (blocks,), jnp.float32, smallest / len(split), largest / len(split))
        gain = gain * jnp.repeat(jnp.exp(heights), shape[position] // blocks).reshape((-1,) + (1,) * (len(shape) - 1 - position))
    return gain


def gaussian(key, dims, scale, bound, split=(), held_as=jnp.bfloat16):
    factor_of = level_of(key, dims, split, -0.22, 0.18) if split else 1.0
    drawn = jax.random.normal(key, dims, jnp.float32) * scale * factor_of
    return jnp.minimum(jnp.maximum(drawn, -bound), bound).astype(held_as)


def setup_inputs(seed: int = 0) -> dict:
    arg_keys = jax.random.split(jax.random.key(seed), 4)
    return {
        "velocity": gaussian(arg_keys[0], (PHASES, 3, NZ, XW, YW), 1.0, 3.0, ((0, 32), (2, 8)), jnp.float32),
        "image": gaussian(arg_keys[1], (PHASES, NZ, XW, YW), 1.0, 6.0, ((0, 32), (1, 8)), jnp.float32),
        "target": gaussian(arg_keys[2], (PHASES, NZ, XW, YW), 1.0, 6.0, ((0, 32), (1, 8)), jnp.float32),
    }


STEP_DT = 0.1
RAW_WEIGHTS = [0.6 ** order for order in range(5)]
WEIGHT_TOTAL = RAW_WEIGHTS[0] + 2.0 * (RAW_WEIGHTS[1] + RAW_WEIGHTS[2] + RAW_WEIGHTS[3] + RAW_WEIGHTS[4])
FRAME_WEIGHTS = [value / WEIGHT_TOTAL for value in RAW_WEIGHTS]


def window_cut(array, dim, start_at, stop_at):
    selector = [slice(None)] * array.ndim
    for other in range(3):
        place = array.ndim - 3 + other
        if other == dim:
            selector[place] = slice(start_at, stop_at)
        else:
            selector[place] = slice(1, array.shape[place] - 1)
    return array[tuple(selector)]


def transport(padded_field, padded_speed):
    result = window_cut(padded_field, 0, 1, padded_field.shape[0] - 1)
    for dim in range(3):
        extent = padded_field.shape[dim] - 2
        lower_cell = window_cut(padded_field, dim, 0, extent + 1)
        upper_cell = window_cut(padded_field, dim, 1, extent + 2)
        face_speed = 0.5 * (window_cut(padded_speed[dim], dim, 0, extent + 1) + window_cut(padded_speed[dim], dim, 1, extent + 2))
        face_flux = jnp.maximum(face_speed, 0.0) * lower_cell + jnp.minimum(face_speed, 0.0) * upper_cell
        divergence = lax.slice_in_dim(face_flux, 1, extent + 1, axis=dim) - lax.slice_in_dim(face_flux, 0, extent, axis=dim)
        result = result - STEP_DT * divergence
    return result


def gradient(padded_image):
    parts = []
    for dim in range(3):
        extent = padded_image.shape[dim] - 2
        parts.append(0.5 * (window_cut(padded_image, dim, 2, extent + 2) - window_cut(padded_image, dim, 0, extent)))
    return jnp.stack(parts)


def reference(velocity, image, target):
    source = image - target
    padded_velocity = jnp.pad(velocity, ((0, 0), (0, 0), (1, 1), (1, 1), (1, 1)))
    adjoint = source
    for step in range(STEPS):
        later = jnp.roll(adjoint, -1, axis=0)
        moved = lax.map(lambda pair: transport(jnp.pad(pair[0], 1), pair[1]), (later, padded_velocity))
        adjoint = source + moved
    grads = lax.map(lambda frame: gradient(jnp.pad(frame, 1)), image)
    descent = velocity - adjoint[:, None] * grads
    smoothed = FRAME_WEIGHTS[0] * descent
    for shift_by in range(1, TAPS + 1):
        smoothed = smoothed + FRAME_WEIGHTS[shift_by] * (jnp.roll(descent, -shift_by, axis=0) + jnp.roll(descent, shift_by, axis=0))
    return adjoint, smoothed
```

```python
import functools

import jax
import jax.numpy as jnp
from jax import lax
from jax.experimental import pallas as pl
from jax.experimental.pallas import tpu as pltpu
from jax.sharding import PartitionSpec as P

MESH = pl.DeviceIdType.MESH
STEPS = 4
TAPS = 4
STEP_DT = 0.1
RAW_WEIGHTS = [0.6**order for order in range(5)]
WEIGHT_TOTAL = RAW_WEIGHTS[0] + 2.0 * (
    RAW_WEIGHTS[1] + RAW_WEIGHTS[2] + RAW_WEIGHTS[3] + RAW_WEIGHTS[4]
)
FRAME_WEIGHTS = [value / WEIGHT_TOTAL for value in RAW_WEIGHTS]

GROUP = 4
QP = 16
XW, YW = 16, 128
HALVES = 2
CP = QP // HALVES


def flip(g):
    return g + 1 - 2 * lax.rem(g, 2)


def kernel(
    phases,
    slabs,
    v_ref,
    img_ref,
    tgt_ref,
    adj_out,
    smo_out,
    img_own,
    tgt_own,
    s_own,
    v0,
    v12,
    img,
    lam,
    lam_in,
    coef,
    adj,
    des,
    des_far,
    smo,
    load_sem,
    in_send,
    in_recv,
    edge_send,
    edge_recv,
    lz_send,
    lz_recv,
    adj_send,
    adj_recv,
    d_send,
    d_recv,
    o_send,
    o_recv,
):
    phase = lax.axis_index("phase")
    slab = lax.axis_index("gz")
    q = lax.rem(phase, GROUP)
    base = phase - q
    upper_base = lax.rem(base + GROUP, phases)
    lower_base = lax.rem(base + phases - GROUP, phases)
    other = flip(slab)
    quarters = slabs * GROUP
    place = other * GROUP + q
    after = lax.rem(place + 1, quarters)
    before = lax.rem(place + quarters - 1, quarters)
    after_q, after_slab = lax.rem(after, GROUP), flip(lax.div(after, GROUP))
    before_q, before_slab = lax.rem(before, GROUP), flip(lax.div(before, GROUP))
    not_first = jnp.where(place == 0, 0.0, 1.0)
    not_last = jnp.where(place == quarters - 1, 0.0, 1.0)

    started = []

    def send(src, dst, send_sem, recv_sem, device):
        copy = pltpu.make_async_remote_copy(
            src_ref=src,
            dst_ref=dst,
            send_sem=send_sem,
            recv_sem=recv_sem,
            device_id=device,
            device_id_type=MESH,
        )
        copy.start()
        started.append(copy)

    def arrived(dst, send_sem, recv_sem):
        pltpu.make_async_remote_copy(
            src_ref=dst,
            dst_ref=dst,
            send_sem=send_sem,
            recv_sem=recv_sem,
            device_id=(phase, slab),
            device_id_type=MESH,
        ).wait_recv()

    loads = [
        pltpu.make_async_copy(img_ref.at[0], img_own, load_sem.at[0]),
        pltpu.make_async_copy(tgt_ref.at[0], tgt_own, load_sem.at[1]),
    ]
    for load in loads:
        load.start()

    partners = [(base + j, other) for j in range(GROUP)]
    partners += [(upper_base + q, slab), (lower_base + q, slab)]
    for here in (base, upper_base, lower_base):
        partners += [(here + after_q, after_slab), (here + before_q, before_slab)]
    barrier = pltpu.get_barrier_semaphore()
    for partner in partners:
        pl.semaphore_signal(barrier, inc=1, device_id=partner, device_id_type=MESH)
    pl.semaphore_wait(barrier, len(partners))

    def scatter(field, source, dest):
        for j in range(GROUP):
            send(
                source(j),
                dest,
                in_send.at[field, j],
                in_recv.at[field, q],
                (base + j, other),
            )

    def gathered(field, dest):
        for i in range(GROUP):
            arrived(dest(i), in_send.at[field, i], in_recv.at[field, i])

    inner = pl.ds(1, QP)
    scatter(0, lambda j: v_ref.at[0, 0, pl.ds(QP * j, QP)], v0.at[q, inner])
    for load in loads:
        load.wait()

    @pl.loop(0, QP)
    def _(t):
        for r in range(GROUP):
            s_own[t * GROUP + r] = img_own[t * GROUP + r] - tgt_own[t * GROUP + r]

    scatter(1, lambda j: s_own.at[pl.ds(QP * j, QP)], lam.at[0, q, inner])
    scatter(2, lambda j: v_ref.at[0, pl.ds(1, 2), pl.ds(QP * j, QP)], v12.at[q])
    scatter(3, lambda j: img_ref.at[0, pl.ds(QP * j, QP)], img.at[q, inner])

    def send_edges(slot, buffer, dest, here):
        send(
            buffer(1),
            dest(QP + 1),
            edge_send.at[slot, 0],
            edge_recv.at[slot, 0],
            (here + before_q, before_slab),
        )
        send(
            buffer(QP),
            dest(0),
            edge_send.at[slot, 1],
            edge_recv.at[slot, 1],
            (here + after_q, after_slab),
        )

    def edges_arrived(slot, dest):
        arrived(dest(QP + 1), edge_send.at[slot, 0], edge_recv.at[slot, 0])
        arrived(dest(0), edge_send.at[slot, 1], edge_recv.at[slot, 1])

    def send_first(k):
        send(
            lam.at[k, 0, inner],
            lam_in.at[k, inner],
            lz_send.at[k],
            lz_recv.at[k],
            (lower_base + q, slab),
        )
        send_edges(
            2 * k,
            lambda plane: lam.at[k, 0, plane],
            lambda plane: lam_in.at[k, plane],
            lower_base,
        )

    def first_arrived(k):
        arrived(lam_in.at[k, inner], lz_send.at[k], lz_recv.at[k])
        edges_arrived(2 * k, lambda plane: lam_in.at[k, plane])

    def rest_edges(k):
        return lambda plane: lam.at[k, pl.ds(1, GROUP - 1), plane]

    def send_rest(k):
        send_edges(2 * k + 1, rest_edges(k), rest_edges(k), base)

    v0_edges = lambda plane: v0.at[:, plane]
    img_edges = lambda plane: img.at[:, plane]
    V_SLOT, IMG_SLOT = 2 * STEPS, 2 * STEPS + 1

    gathered(0, lambda i: v0.at[i, inner])
    send_edges(V_SLOT, v0_edges, v0_edges, base)
    gathered(1, lambda i: lam.at[0, i, inner])
    send_first(0)
    send_rest(0)
    edges_arrived(V_SLOT, v0_edges)
    gathered(2, lambda i: v12.at[i])

    row = lax.broadcasted_iota(jnp.int32, (XW, YW), 0)
    lane = lax.broadcasted_iota(jnp.int32, (XW, YW), 1)

    def shifted(a, axis):
        size = (XW, YW)[axis]
        return pltpu.roll(a, 1, axis), pltpu.roll(a, size - 1, axis)

    dt = STEP_DT
    at_low = (row == 0, lane == 0)
    at_high = (row == XW - 1, lane == YW - 1)

    @pl.loop(0, QP)
    def _(t):
        keep_low = jnp.where(t == 0, not_first, 1.0)
        keep_high = jnp.where(t == QP - 1, not_last, 1.0)
        for i in range(GROUP):
            mid = v0[i, t + 1]
            w_low = 0.5 * (v0[i, t] * keep_low + mid)
            w_high = 0.5 * (v0[i, t + 2] * keep_high + mid)
            total = jnp.maximum(w_high, 0.0) - jnp.minimum(w_low, 0.0)
            coef[i, t, 1] = (dt * keep_low) * jnp.maximum(w_low, 0.0)
            coef[i, t, 2] = (-dt * keep_high) * jnp.minimum(w_high, 0.0)
            for axis in range(2):
                mid = v12[i, axis, t]
                low, high = shifted(mid, axis)
                w_low = 0.5 * (jnp.where(at_low[axis], 0.0, low) + mid)
                w_high = 0.5 * (jnp.where(at_high[axis], 0.0, high) + mid)
                total = total + (jnp.maximum(w_high, 0.0) - jnp.minimum(w_low, 0.0))
                coef[i, t, 3 + 2 * axis] = jnp.where(
                    at_low[axis], 0.0, dt * jnp.maximum(w_low, 0.0)
                )
                coef[i, t, 4 + 2 * axis] = jnp.where(
                    at_high[axis], 0.0, -dt * jnp.minimum(w_high, 0.0)
                )
            coef[i, t, 0] = 1.0 - dt * total

    def transport(i, u_at, store):
        @pl.loop(0, QP // 2)
        def _(pair):
            for r in range(2):
                t = pair * 2 + r
                u = u_at(t + 1)
                x_low, x_high = shifted(u, 0)
                y_low, y_high = shifted(u, 1)
                near = coef[i, t, 0] * u + lam[0, i, t + 1]
                z_part = coef[i, t, 1] * u_at(t) + coef[i, t, 2] * u_at(t + 2)
                x_part = coef[i, t, 3] * x_low + coef[i, t, 4] * x_high
                y_part = coef[i, t, 5] * y_low + coef[i, t, 6] * y_high
                store(t, (near + z_part) + (x_part + y_part))

    for k in range(1, STEPS + 1):
        def result(i):
            def store(t, value):
                if k < STEPS:
                    lam[k, i, t + 1] = value
                else:
                    adj[i, t] = value

            return store

        edges_arrived(2 * k - 1, rest_edges(k - 1))
        for i in range(GROUP - 1):
            transport(i, lambda t: lam[k - 1, i + 1, t], result(i))
            if i == 0 and k < STEPS:
                send_first(k)
        if k == 3:
            gathered(3, lambda i: img.at[i, inner])
            send_edges(IMG_SLOT, img_edges, img_edges, base)
        first_arrived(k - 1)
        transport(GROUP - 1, lambda t: lam_in[k - 1, t], result(GROUP - 1))
        if k < STEPS:
            send_rest(k)

    for i in range(GROUP):
        send(
            adj.at[i],
            adj_out.at[0, pl.ds(QP * q, QP)],
            adj_send.at[i],
            adj_recv.at[q],
            (base + i, other),
        )
    edges_arrived(IMG_SLOT, img_edges)

    chunks = [(dim, half) for dim in range(3) for half in range(HALVES)]
    for number, (dim, half) in enumerate(chunks):
        @pl.loop(0, CP)
        def _(step):
            t = half * CP + step
            for i in range(GROUP):
                if dim == 0:
                    low = img[i, t] * jnp.where(t == 0, not_first, 1.0)
                    high = img[i, t + 2] * jnp.where(t == QP - 1, not_last, 1.0)
                    speed = v0[i, t + 1]
                else:
                    low, high = shifted(img[i, t + 1], dim - 1)
                    low = jnp.where(at_low[dim - 1], 0.0, low)
                    high = jnp.where(at_high[dim - 1], 0.0, high)
                    speed = v12[i, dim - 1, t]
                des[dim, i, t] = speed - adj[i, t] * (0.5 * (high - low))

        part = (dim, slice(None), pl.ds(half * CP, CP))
        for way, there in ((0, upper_base), (1, lower_base)):
            send(
                des.at[part],
                des_far.at[(way,) + part],
                d_send.at[way, number],
                d_recv.at[way, number],
                (there + q, slab),
            )

    for number, (dim, half) in enumerate(chunks):
        part = (dim, slice(None), pl.ds(half * CP, CP))
        for way in range(2):
            arrived(des_far.at[(way,) + part], d_send.at[way, number], d_recv.at[way, number])

        @pl.loop(0, CP)
        def _(step):
            t = half * CP + step
            line = [des_far[0, dim, i, t] for i in range(GROUP)]
            line += [des[dim, i, t] for i in range(GROUP)]
            line += [des_far[1, dim, i, t] for i in range(GROUP)]
            for i in range(GROUP):
                c = GROUP + i
                value = FRAME_WEIGHTS[0] * line[c]
                for k in range(1, TAPS + 1):
                    value = value + FRAME_WEIGHTS[k] * (line[c + k] + line[c - k])
                smo[dim, i, t] = value

        for i in range(GROUP):
            send(
                smo.at[dim, i, pl.ds(half * CP, CP)],
                smo_out.at[0, dim, pl.ds(QP * q + half * CP, CP)],
                o_send.at[number, i],
                o_recv.at[number, q],
                (base + i, other),
            )

    for j in range(GROUP):
        arrived(adj_out.at[0, pl.ds(QP * j, QP)], adj_send.at[j], adj_recv.at[j])
    for number, (dim, half) in enumerate(chunks):
        for j in range(GROUP):
            arrived(
                smo_out.at[0, dim, pl.ds(QP * j + half * CP, CP)],
                o_send.at[number, j],
                o_recv.at[number, j],
            )
    for copy in started:
        copy.wait_send()


def solution(mesh):
    phases, slabs = mesh.shape["phase"], mesh.shape["gz"]

    def local(velocity, image, target):
        f32 = jnp.float32
        vmem = lambda *lead: pltpu.VMEM(lead + (XW, YW), f32)
        dma = pltpu.SemaphoreType.DMA
        planes = image.shape[1]
        chunks = 3 * HALVES
        anywhere = pl.BlockSpec(memory_space=pl.ANY)
        return pl.pallas_call(
            functools.partial(kernel, phases, slabs),
            out_shape=(
                jax.ShapeDtypeStruct(image.shape, f32),
                jax.ShapeDtypeStruct(velocity.shape, f32),
            ),
            in_specs=[anywhere] * 3,
            out_specs=(anywhere, anywhere),
            scratch_shapes=[
                vmem(planes),
                vmem(planes),
                vmem(planes),
                vmem(GROUP, QP + 2),
                vmem(GROUP, 2, QP),
                vmem(GROUP, QP + 2),
                vmem(STEPS, GROUP, QP + 2),
                vmem(STEPS, QP + 2),
                vmem(GROUP, QP, 7),
                vmem(GROUP, QP),
                vmem(3, GROUP, QP),
                vmem(2, 3, GROUP, QP),
                vmem(3, GROUP, QP),
                dma((2,)),
                dma((4, GROUP)),
                dma((4, GROUP)),
                dma((2 * STEPS + 2, 2)),
                dma((2 * STEPS + 2, 2)),
                dma((STEPS,)),
                dma((STEPS,)),
                dma((GROUP,)),
                dma((GROUP,)),
                dma((2, chunks)),
                dma((2, chunks)),
                dma((chunks, GROUP)),
                dma((chunks, GROUP)),
            ],
            compiler_params=pltpu.CompilerParams(
                collective_id=0,
                has_side_effects=True,
                vmem_limit_bytes=40 * 1024 * 1024,
            ),
        )(velocity, image, target)

    return jax.shard_map(
        local,
        mesh=mesh,
        in_specs=(
            P("phase", None, "gz", None, None),
            P("phase", "gz", None, None),
            P("phase", "gz", None, None),
        ),
        out_specs=(P("phase", "gz", None, None), P("phase", None, "gz", None, None)),
        check_vma=False,
    )
```

```python
import functools

import jax
import jax.numpy as jnp
from jax import lax
from jax.experimental import pallas as pl
from jax.experimental.pallas import tpu as pltpu
from jax.sharding import PartitionSpec as P

MESH = pl.DeviceIdType.MESH
STEPS = 4
TAPS = 4
STEP_DT = 0.1
RAW_WEIGHTS = [0.6**order for order in range(5)]
WEIGHT_TOTAL = RAW_WEIGHTS[0] + 2.0 * (
    RAW_WEIGHTS[1] + RAW_WEIGHTS[2] + RAW_WEIGHTS[3] + RAW_WEIGHTS[4]
)
FRAME_WEIGHTS = [value / WEIGHT_TOTAL for value in RAW_WEIGHTS]

GROUP = 4
QP = 16
XW, YW = 16, 128
HALVES = 2
CP = QP // HALVES


def flip(g):
    return g + 1 - 2 * lax.rem(g, 2)


def kernel(
    phases,
    slabs,
    v_ref,
    img_ref,
    tgt_ref,
    adj_out,
    smo_out,
    img_own,
    tgt_own,
    s_own,
    v0,
    v12,
    img,
    lam,
    lam_in,
    coef,
    adj,
    des,
    des_far,
    smo,
    load_sem,
    in_send,
    in_recv,
    edge_send,
    edge_recv,
    lz_send,
    lz_recv,
    adj_send,
    adj_recv,
    d_send,
    d_recv,
    o_send,
    o_recv,
):
    phase = lax.axis_index("phase")
    slab = lax.axis_index("gz")
    q = lax.rem(phase, GROUP)
    base = phase - q
    upper_base = lax.rem(base + GROUP, phases)
    lower_base = lax.rem(base + phases - GROUP, phases)
    other = flip(slab)
    quarters = slabs * GROUP
    place = other * GROUP + q
    after = lax.rem(place + 1, quarters)
    before = lax.rem(place + quarters - 1, quarters)
    after_q, after_slab = lax.rem(after, GROUP), flip(lax.div(after, GROUP))
    before_q, before_slab = lax.rem(before, GROUP), flip(lax.div(before, GROUP))
    not_first = jnp.where(place == 0, 0.0, 1.0)
    not_last = jnp.where(place == quarters - 1, 0.0, 1.0)

    started = []

    def send(src, dst, send_sem, recv_sem, device):
        copy = pltpu.make_async_remote_copy(
            src_ref=src,
            dst_ref=dst,
            send_sem=send_sem,
            recv_sem=recv_sem,
            device_id=device,
            device_id_type=MESH,
        )
        copy.start()
        started.append(copy)

    def arrived(dst, send_sem, recv_sem):
        pltpu.make_async_remote_copy(
            src_ref=dst,
            dst_ref=dst,
            send_sem=send_sem,
            recv_sem=recv_sem,
            device_id=(phase, slab),
            device_id_type=MESH,
        ).wait_recv()

    loads = [
        pltpu.make_async_copy(img_ref.at[0], img_own, load_sem.at[0]),
        pltpu.make_async_copy(tgt_ref.at[0], tgt_own, load_sem.at[1]),
    ]
    for load in loads:
        load.start()

    partners = [(base + j, other) for j in range(GROUP)]
    partners += [(upper_base + q, slab), (lower_base + q, slab)]
    for here in (base, upper_base, lower_base):
        partners += [(here + after_q, after_slab), (here + before_q, before_slab)]
    barrier = pltpu.get_barrier_semaphore()
    for partner in partners:
        pl.semaphore_signal(barrier, inc=1, device_id=partner, device_id_type=MESH)
    pl.semaphore_wait(barrier, len(partners))

    def scatter(field, source, dest):
        for j in range(GROUP):
            send(
                source(j),
                dest,
                in_send.at[field, j],
                in_recv.at[field, q],
                (base + j, other),
            )

    def gathered(field, dest):
        for i in range(GROUP):
            arrived(dest(i), in_send.at[field, i], in_recv.at[field, i])

    inner = pl.ds(1, QP)
    scatter(0, lambda j: v_ref.at[0, 0, pl.ds(QP * j, QP)], v0.at[q, inner])
    for load in loads:
        load.wait()

    @pl.loop(0, QP)
    def _(t):
        for r in range(GROUP):
            s_own[t * GROUP + r] = img_own[t * GROUP + r] - tgt_own[t * GROUP + r]

    scatter(1, lambda j: s_own.at[pl.ds(QP * j, QP)], lam.at[0, q, inner])
    scatter(2, lambda j: v_ref.at[0, pl.ds(1, 2), pl.ds(QP * j, QP)], v12.at[q])
    scatter(3, lambda j: img_ref.at[0, pl.ds(QP * j, QP)], img.at[q, inner])

    def send_edges(slot, buffer, dest, here):
        send(
            buffer(1),
            dest(QP + 1),
            edge_send.at[slot, 0],
            edge_recv.at[slot, 0],
            (here + before_q, before_slab),
        )
        send(
            buffer(QP),
            dest(0),
            edge_send.at[slot, 1],
            edge_recv.at[slot, 1],
            (here + after_q, after_slab),
        )

    def edges_arrived(slot, dest):
        arrived(dest(QP + 1), edge_send.at[slot, 0], edge_recv.at[slot, 0])
        arrived(dest(0), edge_send.at[slot, 1], edge_recv.at[slot, 1])

    def send_main(k):
        send(
            lam.at[k, 0, inner],
            lam_in.at[k, inner],
            lz_send.at[k],
            lz_recv.at[k],
            (lower_base + q, slab),
        )

    def lam_edges(k, i):
        if i == 0:
            return lambda plane: lam_in.at[k, plane]
        return lambda plane: lam.at[k, i, plane]

    def send_lam_edges(k, i):
        send_edges(
            GROUP * k + i,
            lambda plane: lam.at[k, i, plane],
            lam_edges(k, i),
            lower_base if i == 0 else base,
        )

    def lam_edges_arrived(k, i):
        edges_arrived(GROUP * k + i, lam_edges(k, i))

    v0_edges = lambda plane: v0.at[:, plane]
    img_edges = lambda plane: img.at[:, plane]
    V_SLOT, IMG_SLOT = GROUP * STEPS, GROUP * STEPS + 1

    gathered(0, lambda i: v0.at[i, inner])
    send_edges(V_SLOT, v0_edges, v0_edges, base)
    gathered(1, lambda i: lam.at[0, i, inner])
    send_main(0)
    for i in range(GROUP):
        send_lam_edges(0, i)
    edges_arrived(V_SLOT, v0_edges)
    gathered(2, lambda i: v12.at[i])

    row = lax.broadcasted_iota(jnp.int32, (XW, YW), 0)
    lane = lax.broadcasted_iota(jnp.int32, (XW, YW), 1)

    def shifted(a, axis):
        size = (XW, YW)[axis]
        return pltpu.roll(a, 1, axis), pltpu.roll(a, size - 1, axis)

    dt = STEP_DT
    at_low = (row == 0, lane == 0)
    at_high = (row == XW - 1, lane == YW - 1)

    @pl.loop(0, QP)
    def _(t):
        keep_low = jnp.where(t == 0, not_first, 1.0)
        keep_high = jnp.where(t == QP - 1, not_last, 1.0)
        for i in range(GROUP):
            mid = v0[i, t + 1]
            w_low = 0.5 * (v0[i, t] * keep_low + mid)
            w_high = 0.5 * (v0[i, t + 2] * keep_high + mid)
            total = jnp.maximum(w_high, 0.0) - jnp.minimum(w_low, 0.0)
            coef[i, t, 1] = (dt * keep_low) * jnp.maximum(w_low, 0.0)
            coef[i, t, 2] = (-dt * keep_high) * jnp.minimum(w_high, 0.0)
            for axis in range(2):
                mid = v12[i, axis, t]
                low, high = shifted(mid, axis)
                w_low = 0.5 * (jnp.where(at_low[axis], 0.0, low) + mid)
                w_high = 0.5 * (jnp.where(at_high[axis], 0.0, high) + mid)
                total = total + (jnp.maximum(w_high, 0.0) - jnp.minimum(w_low, 0.0))
                coef[i, t, 3 + 2 * axis] = jnp.where(
                    at_low[axis], 0.0, dt * jnp.maximum(w_low, 0.0)
                )
                coef[i, t, 4 + 2 * axis] = jnp.where(
                    at_high[axis], 0.0, -dt * jnp.minimum(w_high, 0.0)
                )
            coef[i, t, 0] = 1.0 - dt * total

    def transport(i, t, u_at, store):
        u = u_at(t + 1)
        x_low, x_high = shifted(u, 0)
        y_low, y_high = shifted(u, 1)
        near = coef[i, t, 0] * u + lam[0, i, t + 1]
        z_part = coef[i, t, 1] * u_at(t) + coef[i, t, 2] * u_at(t + 2)
        x_part = coef[i, t, 3] * x_low + coef[i, t, 4] * x_high
        y_part = coef[i, t, 5] * y_low + coef[i, t, 6] * y_high
        store(t, (near + z_part) + (x_part + y_part))

    def advance(k, i):
        def u_at(plane):
            return lam_in[k - 1, plane] if i == GROUP - 1 else lam[k - 1, i + 1, plane]

        def store(t, value):
            if k < STEPS:
                lam[k, i, t + 1] = value
            else:
                adj[i, t] = value

        if i == GROUP - 1:
            arrived(lam_in.at[k - 1, inner], lz_send.at[k - 1], lz_recv.at[k - 1])
        lam_edges_arrived(k - 1, (i + 1) % GROUP)
        for t in (0, QP - 1):
            transport(i, t, u_at, store)
        if k < STEPS:
            send_lam_edges(k, i)

        @pl.loop(0, 2)
        def _(part):
            for r in range(QP // 2 - 1):
                transport(i, 1 + part * (QP // 2 - 1) + r, u_at, store)

        if k < STEPS and i == 0:
            send_main(k)

    order = (
        [(1, 0), (1, 1), (1, 2), (1, 3), (2, 0), (2, 1), (2, 2), (3, 0), (3, 1), (2, 3)]
        + [(4, 0), (3, 2), (3, 3), (4, 1), (4, 2), (4, 3)]
    )
    for k, i in order:
        if (k, i) == (2, 3):
            gathered(3, lambda i: img.at[i, inner])
            send_edges(IMG_SLOT, img_edges, img_edges, base)
        advance(k, i)

    for i in range(GROUP):
        send(
            adj.at[i],
            adj_out.at[0, pl.ds(QP * q, QP)],
            adj_send.at[i],
            adj_recv.at[q],
            (base + i, other),
        )
    edges_arrived(IMG_SLOT, img_edges)

    chunks = [(dim, half) for dim in range(3) for half in range(HALVES)]
    for number, (dim, half) in enumerate(chunks):
        @pl.loop(0, CP // 4)
        def _(step):
            for t, i in [(half * CP + step * 4 + r, i) for r in range(4) for i in range(GROUP)]:
                if dim == 0:
                    low = img[i, t] * jnp.where(t == 0, not_first, 1.0)
                    high = img[i, t + 2] * jnp.where(t == QP - 1, not_last, 1.0)
                    speed = v0[i, t + 1]
                else:
                    low, high = shifted(img[i, t + 1], dim - 1)
                    low = jnp.where(at_low[dim - 1], 0.0, low)
                    high = jnp.where(at_high[dim - 1], 0.0, high)
                    speed = v12[i, dim - 1, t]
                des[dim, i, t] = speed - adj[i, t] * (0.5 * (high - low))

        part = (dim, slice(None), pl.ds(half * CP, CP))
        for way, there in ((0, upper_base), (1, lower_base)):
            send(
                des.at[part],
                des_far.at[(way,) + part],
                d_send.at[way, number],
                d_recv.at[way, number],
                (there + q, slab),
            )

    for number, (dim, half) in enumerate(chunks):
        part = (dim, slice(None), pl.ds(half * CP, CP))
        for way in range(2):
            arrived(des_far.at[(way,) + part], d_send.at[way, number], d_recv.at[way, number])

        @pl.loop(0, CP // 2)
        def _(step):
            for r in range(2):
                t = half * CP + step * 2 + r
                line = [des_far[0, dim, i, t] for i in range(GROUP)]
                line += [des[dim, i, t] for i in range(GROUP)]
                line += [des_far[1, dim, i, t] for i in range(GROUP)]
                for i in range(GROUP):
                    c = GROUP + i
                    value = FRAME_WEIGHTS[0] * line[c]
                    for k in range(1, TAPS + 1):
                        value = value + FRAME_WEIGHTS[k] * (line[c + k] + line[c - k])
                    smo[dim, i, t] = value

        for i in range(GROUP):
            send(
                smo.at[dim, i, pl.ds(half * CP, CP)],
                smo_out.at[0, dim, pl.ds(QP * q + half * CP, CP)],
                o_send.at[number, i],
                o_recv.at[number, q],
                (base + i, other),
            )

    for j in range(GROUP):
        arrived(adj_out.at[0, pl.ds(QP * j, QP)], adj_send.at[j], adj_recv.at[j])
    for number, (dim, half) in enumerate(chunks):
        for j in range(GROUP):
            arrived(
                smo_out.at[0, dim, pl.ds(QP * j + half * CP, CP)],
                o_send.at[number, j],
                o_recv.at[number, j],
            )
    for copy in started:
        copy.wait_send()


def solution(mesh):
    phases, slabs = mesh.shape["phase"], mesh.shape["gz"]

    def local(velocity, image, target):
        f32 = jnp.float32
        vmem = lambda *lead: pltpu.VMEM(lead + (XW, YW), f32)
        dma = pltpu.SemaphoreType.DMA
        planes = image.shape[1]
        chunks = 3 * HALVES
        anywhere = pl.BlockSpec(memory_space=pl.ANY)
        return pl.pallas_call(
            functools.partial(kernel, phases, slabs),
            out_shape=(
                jax.ShapeDtypeStruct(image.shape, f32),
                jax.ShapeDtypeStruct(velocity.shape, f32),
            ),
            in_specs=[anywhere] * 3,
            out_specs=(anywhere, anywhere),
            scratch_shapes=[
                vmem(planes),
                vmem(planes),
                vmem(planes),
                vmem(GROUP, QP + 2),
                vmem(GROUP, 2, QP),
                vmem(GROUP, QP + 2),
                vmem(STEPS, GROUP, QP + 2),
                vmem(STEPS, QP + 2),
                vmem(GROUP, QP, 7),
                vmem(GROUP, QP),
                vmem(3, GROUP, QP),
                vmem(2, 3, GROUP, QP),
                vmem(3, GROUP, QP),
                dma((2,)),
                dma((4, GROUP)),
                dma((4, GROUP)),
                dma((GROUP * STEPS + 2, 2)),
                dma((GROUP * STEPS + 2, 2)),
                dma((STEPS,)),
                dma((STEPS,)),
                dma((GROUP,)),
                dma((GROUP,)),
                dma((2, chunks)),
                dma((2, chunks)),
                dma((chunks, GROUP)),
                dma((chunks, GROUP)),
            ],
            compiler_params=pltpu.CompilerParams(
                collective_id=0,
                has_side_effects=True,
                vmem_limit_bytes=40 * 1024 * 1024,
            ),
        )(*(pltpu.with_memory_space_constraint(a, pltpu.HBM) for a in (velocity, image, target)))

    return jax.shard_map(
        local,
        mesh=mesh,
        in_specs=(
            P("phase", None, "gz", None, None),
            P("phase", "gz", None, None),
            P("phase", "gz", None, None),
        ),
        out_specs=(P("phase", "gz", None, None), P("phase", None, "gz", None, None)),
        check_vma=False,
    )
```

```python
import functools

import jax
import jax.numpy as jnp
from jax import lax
from jax.experimental import pallas as pl
from jax.experimental.pallas import tpu as pltpu
from jax.sharding import PartitionSpec as P

MESH = pl.DeviceIdType.MESH
STEPS = 4
TAPS = 4
STEP_DT = 0.1
RAW_WEIGHTS = [0.6**order for order in range(5)]
WEIGHT_TOTAL = RAW_WEIGHTS[0] + 2.0 * (
    RAW_WEIGHTS[1] + RAW_WEIGHTS[2] + RAW_WEIGHTS[3] + RAW_WEIGHTS[4]
)
FRAME_WEIGHTS = [value / WEIGHT_TOTAL for value in RAW_WEIGHTS]

GROUP = 4
QP = 16
XW, YW = 16, 128
EARLY = QP // 2
CP = 4
PIECE = 2


def flip(g):
    return g + 1 - 2 * lax.rem(g, 2)


def kernel(
    phases,
    slabs,
    v_ref,
    img_ref,
    tgt_ref,
    adj_out,
    smo_out,
    img_own,
    tgt_own,
    s_own,
    vel,
    img,
    lam,
    lam_in,
    coef,
    adj,
    des,
    des_far,
    vel_far,
    img_far,
    adj_far,
    smo,
    load_sem,
    in_send,
    in_recv,
    edge_send,
    edge_recv,
    lz_send,
    lz_recv,
    adj_send,
    adj_recv,
    d_send,
    d_recv,
    o_send,
    o_recv,
):
    phase = lax.axis_index("phase")
    slab = lax.axis_index("gz")
    q = lax.rem(phase, GROUP)
    base = phase - q
    upper_base = lax.rem(base + GROUP, phases)
    lower_base = lax.rem(base + phases - GROUP, phases)
    other = flip(slab)
    quarters = slabs * GROUP
    place = other * GROUP + q
    after = lax.rem(place + 1, quarters)
    before = lax.rem(place + quarters - 1, quarters)
    after_q, after_slab = lax.rem(after, GROUP), flip(lax.div(after, GROUP))
    before_q, before_slab = lax.rem(before, GROUP), flip(lax.div(before, GROUP))
    not_first = jnp.where(place == 0, 0.0, 1.0)
    not_last = jnp.where(place == quarters - 1, 0.0, 1.0)

    started = []

    def send(src, dst, send_sem, recv_sem, device):
        copy = pltpu.make_async_remote_copy(
            src_ref=src,
            dst_ref=dst,
            send_sem=send_sem,
            recv_sem=recv_sem,
            device_id=device,
            device_id_type=MESH,
        )
        copy.start()
        started.append(copy)

    def arrived(dst, send_sem, recv_sem):
        pltpu.make_async_remote_copy(
            src_ref=dst,
            dst_ref=dst,
            send_sem=send_sem,
            recv_sem=recv_sem,
            device_id=(phase, slab),
            device_id_type=MESH,
        ).wait_recv()

    loads = [
        pltpu.make_async_copy(img_ref.at[0], img_own, load_sem.at[0]),
        pltpu.make_async_copy(tgt_ref.at[0], tgt_own, load_sem.at[1]),
    ]
    for load in loads:
        load.start()

    partners = [(base + j, other) for j in range(GROUP)]
    partners += [(upper_base + q, slab), (lower_base + q, slab)]
    for here in (base, upper_base, lower_base):
        partners += [(here + after_q, after_slab), (here + before_q, before_slab)]
    barrier = pltpu.get_barrier_semaphore()
    for partner in partners:
        pl.semaphore_signal(barrier, inc=1, device_id=partner, device_id_type=MESH)
    pl.semaphore_wait(barrier, len(partners))

    def scatter(field, source, dest):
        for j in range(GROUP):
            send(
                source(j),
                dest,
                in_send.at[field, j],
                in_recv.at[field, q],
                (base + j, other),
            )

    def gathered(field, dest):
        for i in range(GROUP):
            arrived(dest(i), in_send.at[field, i], in_recv.at[field, i])

    inner = pl.ds(1, QP)
    scatter(0, lambda j: v_ref.at[0, 0, pl.ds(QP * j, QP)], vel.at[q, 0, inner])
    for axis in (1, 2):
        scatter(
            axis,
            lambda j: v_ref.at[0, axis, pl.ds(QP * j, EARLY)],
            vel.at[q, axis, pl.ds(1, EARLY)],
        )
    for load in loads:
        load.wait()

    @pl.loop(0, QP)
    def _(t):
        for r in range(GROUP):
            s_own[t * GROUP + r] = img_own[t * GROUP + r] - tgt_own[t * GROUP + r]

    scatter(3, lambda j: s_own.at[pl.ds(QP * j, QP)], lam.at[0, q, inner])
    late = pl.ds(1 + EARLY, QP - EARLY)
    scatter(
        4,
        lambda j: v_ref.at[0, pl.ds(1, 2), pl.ds(QP * j + EARLY, QP - EARLY)],
        vel.at[q, pl.ds(1, 2), late],
    )

    def scatter_image(piece):
        scatter(
            5 + piece,
            lambda j: img_ref.at[0, pl.ds(QP * j + PIECE * piece, PIECE)],
            img.at[q, pl.ds(1 + PIECE * piece, PIECE)],
        )

    def forward(number, source, dest, ways=(0, 1)):
        for way in ways:
            send(
                source,
                dest(way),
                d_send.at[way, number],
                d_recv.at[way, number],
                ((upper_base, lower_base)[way] + q, slab),
            )

    def forwarded(number, dest):
        for way in range(2):
            arrived(dest(way), d_send.at[way, number], d_recv.at[way, number])

    def send_edges(slot, buffer, dest, here):
        send(
            buffer(1),
            dest(QP + 1),
            edge_send.at[slot, 0],
            edge_recv.at[slot, 0],
            (here + before_q, before_slab),
        )
        send(
            buffer(QP),
            dest(0),
            edge_send.at[slot, 1],
            edge_recv.at[slot, 1],
            (here + after_q, after_slab),
        )

    def edges_arrived(slot, dest):
        arrived(dest(QP + 1), edge_send.at[slot, 0], edge_recv.at[slot, 0])
        arrived(dest(0), edge_send.at[slot, 1], edge_recv.at[slot, 1])

    def send_main(k):
        send(
            lam.at[k, 0, inner],
            lam_in.at[k, inner],
            lz_send.at[k],
            lz_recv.at[k],
            (lower_base + q, slab),
        )

    def lam_edges(k, i):
        if i == 0:
            return lambda plane: lam_in.at[k, plane]
        return lambda plane: lam.at[k, i, plane]

    def send_lam_edges(k, i):
        send_edges(
            GROUP * k + i,
            lambda plane: lam.at[k, i, plane],
            lam_edges(k, i),
            lower_base if i == 0 else base,
        )

    def lam_edges_arrived(k, i):
        edges_arrived(GROUP * k + i, lam_edges(k, i))

    v0_edges = lambda plane: vel.at[:, 0, plane]
    img_edges = lambda plane: img.at[:, plane]
    V_SLOT, IMG_SLOT = GROUP * STEPS, GROUP * STEPS + 1

    def forward_velocity(axis, ways):
        forward(
            axis, vel.at[:, axis, pl.ds(1, EARLY)], lambda way: vel_far.at[way, :, axis], ways
        )

    gathered(0, lambda i: vel.at[i, 0, inner])
    forward_velocity(0, (0, 1))
    send_edges(V_SLOT, v0_edges, v0_edges, base)
    gathered(1, lambda i: vel.at[i, 1, pl.ds(1, EARLY)])
    forward_velocity(1, (0, 1))
    gathered(2, lambda i: vel.at[i, 2, pl.ds(1, EARLY)])
    forward_velocity(2, (0,))
    gathered(3, lambda i: lam.at[0, i, inner])
    send_main(0)
    for i in range(GROUP):
        send_lam_edges(0, i)
    forward_velocity(2, (1,))
    edges_arrived(V_SLOT, v0_edges)
    gathered(4, lambda i: vel.at[i, pl.ds(1, 2), late])

    row = lax.broadcasted_iota(jnp.int32, (XW, YW), 0)
    lane = lax.broadcasted_iota(jnp.int32, (XW, YW), 1)

    def shifted(a, axis):
        size = (XW, YW)[axis]
        return pltpu.roll(a, 1, axis), pltpu.roll(a, size - 1, axis)

    dt = STEP_DT
    at_low = (row == 0, lane == 0)
    at_high = (row == XW - 1, lane == YW - 1)

    @pl.loop(0, QP)
    def _(t):
        keep_low = jnp.where(t == 0, not_first, 1.0)
        keep_high = jnp.where(t == QP - 1, not_last, 1.0)
        for i in range(GROUP):
            mid = vel[i, 0, t + 1]
            w_low = 0.5 * (vel[i, 0, t] * keep_low + mid)
            w_high = 0.5 * (vel[i, 0, t + 2] * keep_high + mid)
            total = jnp.maximum(w_high, 0.0) - jnp.minimum(w_low, 0.0)
            coef[i, t, 1] = (dt * keep_low) * jnp.maximum(w_low, 0.0)
            coef[i, t, 2] = (-dt * keep_high) * jnp.minimum(w_high, 0.0)
            for axis in range(2):
                mid = vel[i, axis + 1, t + 1]
                low, high = shifted(mid, axis)
                w_low = 0.5 * (jnp.where(at_low[axis], 0.0, low) + mid)
                w_high = 0.5 * (jnp.where(at_high[axis], 0.0, high) + mid)
                total = total + (jnp.maximum(w_high, 0.0) - jnp.minimum(w_low, 0.0))
                coef[i, t, 3 + 2 * axis] = jnp.where(
                    at_low[axis], 0.0, dt * jnp.maximum(w_low, 0.0)
                )
                coef[i, t, 4 + 2 * axis] = jnp.where(
                    at_high[axis], 0.0, -dt * jnp.minimum(w_high, 0.0)
                )
            coef[i, t, 0] = 1.0 - dt * total

    def transport(i, t, u_at, store):
        u = u_at(t + 1)
        x_low, x_high = shifted(u, 0)
        y_low, y_high = shifted(u, 1)
        near = coef[i, t, 0] * u + lam[0, i, t + 1]
        z_part = coef[i, t, 1] * u_at(t) + coef[i, t, 2] * u_at(t + 2)
        x_part = coef[i, t, 3] * x_low + coef[i, t, 4] * x_high
        y_part = coef[i, t, 5] * y_low + coef[i, t, 6] * y_high
        store(t, (near + z_part) + (x_part + y_part))

    def advance(k, i):
        def u_at(plane):
            return lam_in[k - 1, plane] if i == GROUP - 1 else lam[k - 1, i + 1, plane]

        def store(t, value):
            if k < STEPS:
                lam[k, i, t + 1] = value
            else:
                adj[i, t] = value

        if i == GROUP - 1:
            arrived(lam_in.at[k - 1, inner], lz_send.at[k - 1], lz_recv.at[k - 1])
        lam_edges_arrived(k - 1, (i + 1) % GROUP)
        for t in (0, QP - 1):
            transport(i, t, u_at, store)
        if k < STEPS:
            send_lam_edges(k, i)

        @pl.loop(0, 2)
        def _(part):
            for r in range(QP // 2 - 1):
                transport(i, 1 + part * (QP // 2 - 1) + r, u_at, store)

        if k < STEPS and i == 0:
            send_main(k)

    order = (
        [(1, 0), (1, 1), (1, 2), (1, 3), (2, 0), (2, 1), (2, 2), (3, 0), (3, 1), (2, 3)]
        + [(4, 0), (3, 2), (3, 3), (4, 1), (4, 2), (4, 3)]
    )
    pieces = QP // PIECE
    near_image = pl.ds(0, EARLY + 2)
    for turn, (k, i) in enumerate(order):
        advance(k, i)
        if turn < pieces:
            scatter_image(turn)
        if (k, i) == (3, 2):
            for piece in range(pieces):
                gathered(5 + piece, lambda i: img.at[i, pl.ds(1 + PIECE * piece, PIECE)])
            send_edges(IMG_SLOT, img_edges, img_edges, base)
        if (k, i) == (4, 1):
            edges_arrived(IMG_SLOT, img_edges)
            forward(3, img.at[:, near_image], lambda way: img_far.at[way])

    forward(4, adj.at[:, pl.ds(0, EARLY)], lambda way: adj_far.at[way])
    for i in range(GROUP):
        send(
            adj.at[i],
            adj_out.at[0, pl.ds(QP * q, QP)],
            adj_send.at[i],
            adj_recv.at[q],
            (base + i, other),
        )

    def descent(image_at, speed, state, dim, t):
        if dim == 0:
            low = image_at(t) * jnp.where(t == 0, not_first, 1.0)
            high = image_at(t + 2) * jnp.where(t == QP - 1, not_last, 1.0)
        else:
            low, high = shifted(image_at(t + 1), dim - 1)
            low = jnp.where(at_low[dim - 1], 0.0, low)
            high = jnp.where(at_high[dim - 1], 0.0, high)
        return speed - state * (0.5 * (high - low))

    def own_descent(dim, start, count):
        @pl.loop(0, count // 4)
        def _(step):
            for r in range(4):
                t = start + step * 4 + r
                for i in range(GROUP):
                    des[dim, i, t] = descent(
                        lambda plane: img[i, plane], vel[i, dim, t + 1], adj[i, t], dim, t
                    )

    def smooth(number, dim, start, count):
        @pl.loop(0, count // 2)
        def _(step):
            for r in range(2):
                t = start + step * 2 + r
                line = [des_far[0, dim, i, t] for i in range(GROUP)]
                line += [des[dim, i, t] for i in range(GROUP)]
                line += [des_far[1, dim, i, t] for i in range(GROUP)]
                for i in range(GROUP):
                    c = GROUP + i
                    value = FRAME_WEIGHTS[0] * line[c]
                    for k in range(1, TAPS + 1):
                        value = value + FRAME_WEIGHTS[k] * (line[c + k] + line[c - k])
                    smo[dim, i, t] = value

        for i in range(GROUP):
            send(
                smo.at[dim, i, pl.ds(start, count)],
                smo_out.at[0, dim, pl.ds(QP * q + start, count)],
                o_send.at[number, i],
                o_recv.at[number, q],
                (base + i, other),
            )

    early_chunks = [(dim, 0, EARLY) for dim in range(3)]
    late_chunks = [(dim, start, CP) for dim in range(3) for start in range(EARLY, QP, CP)]
    chunks = early_chunks + late_chunks
    for number, (dim, start, count) in enumerate(late_chunks):
        own_descent(dim, start, count)
        part = (dim, slice(None), pl.ds(start, count))
        forward(5 + number, des.at[part], lambda way: des_far.at[(way,) + part])
    for dim in range(3):
        own_descent(dim, 0, EARLY)

    for axis in range(3):
        forwarded(axis, lambda way: vel_far.at[way, :, axis])
    forwarded(3, lambda way: img_far.at[way])
    forwarded(4, lambda way: adj_far.at[way])
    for number, (dim, start, count) in enumerate(early_chunks):
        for way in range(2):
            @pl.loop(0, EARLY // 4)
            def _(step):
                for r in range(4):
                    t = step * 4 + r
                    for i in range(GROUP):
                        des_far[way, dim, i, t] = descent(
                            lambda plane: img_far[way, i, plane],
                            vel_far[way, i, dim, t],
                            adj_far[way, i, t],
                            dim,
                            t,
                        )

        smooth(number, dim, start, count)
    for number, (dim, start, count) in enumerate(late_chunks):
        part = (dim, slice(None), pl.ds(start, count))
        forwarded(5 + number, lambda way: des_far.at[(way,) + part])
        smooth(len(early_chunks) + number, dim, start, count)

    for j in range(GROUP):
        arrived(adj_out.at[0, pl.ds(QP * j, QP)], adj_send.at[j], adj_recv.at[j])
    for number, (dim, start, count) in enumerate(chunks):
        for j in range(GROUP):
            arrived(
                smo_out.at[0, dim, pl.ds(QP * j + start, count)],
                o_send.at[number, j],
                o_recv.at[number, j],
            )
    for copy in started:
        copy.wait_send()


def solution(mesh):
    phases, slabs = mesh.shape["phase"], mesh.shape["gz"]

    def local(velocity, image, target):
        f32 = jnp.float32
        vmem = lambda *lead: pltpu.VMEM(lead + (XW, YW), f32)
        dma = pltpu.SemaphoreType.DMA
        planes = image.shape[1]
        late_chunks = 3 * (QP - EARLY) // CP
        chunks = 3 + late_chunks
        fields = 5 + QP // PIECE
        anywhere = pl.BlockSpec(memory_space=pl.ANY)
        return pl.pallas_call(
            functools.partial(kernel, phases, slabs),
            out_shape=(
                jax.ShapeDtypeStruct(image.shape, f32),
                jax.ShapeDtypeStruct(velocity.shape, f32),
            ),
            in_specs=[anywhere] * 3,
            out_specs=(anywhere, anywhere),
            scratch_shapes=[
                vmem(planes),
                vmem(planes),
                vmem(planes),
                vmem(GROUP, 3, QP + 2),
                vmem(GROUP, QP + 2),
                vmem(STEPS, GROUP, QP + 2),
                vmem(STEPS, QP + 2),
                vmem(GROUP, QP, 7),
                vmem(GROUP, QP),
                vmem(3, GROUP, QP),
                vmem(2, 3, GROUP, QP),
                vmem(2, GROUP, 3, EARLY),
                vmem(2, GROUP, EARLY + 2),
                vmem(2, GROUP, EARLY),
                vmem(3, GROUP, QP),
                dma((2,)),
                dma((fields, GROUP)),
                dma((fields, GROUP)),
                dma((GROUP * STEPS + 2, 2)),
                dma((GROUP * STEPS + 2, 2)),
                dma((STEPS,)),
                dma((STEPS,)),
                dma((GROUP,)),
                dma((GROUP,)),
                dma((2, 5 + late_chunks)),
                dma((2, 5 + late_chunks)),
                dma((chunks, GROUP)),
                dma((chunks, GROUP)),
            ],
            compiler_params=pltpu.CompilerParams(
                collective_id=0,
                has_side_effects=True,
                vmem_limit_bytes=40 * 1024 * 1024,
            ),
        )(*(pltpu.with_memory_space_constraint(a, pltpu.HBM) for a in (velocity, image, target)))

    return jax.shard_map(
        local,
        mesh=mesh,
        in_specs=(
            P("phase", None, "gz", None, None),
            P("phase", "gz", None, None),
            P("phase", "gz", None, None),
        ),
        out_specs=(P("phase", "gz", None, None), P("phase", None, "gz", None, None)),
        check_vma=False,
    )
```

```python
import functools

import jax
import jax.numpy as jnp
from jax import lax
from jax.experimental import pallas as pl
from jax.experimental.pallas import tpu as pltpu
from jax.sharding import PartitionSpec as P

MESH = pl.DeviceIdType.MESH
STEPS = 4
TAPS = 4
STEP_DT = 0.1
RAW_WEIGHTS = [0.6**order for order in range(5)]
WEIGHT_TOTAL = RAW_WEIGHTS[0] + 2.0 * (
    RAW_WEIGHTS[1] + RAW_WEIGHTS[2] + RAW_WEIGHTS[3] + RAW_WEIGHTS[4]
)
FRAME_WEIGHTS = [value / WEIGHT_TOTAL for value in RAW_WEIGHTS]

GROUP = 4
QP = 16
XW, YW = 16, 128
EARLY = QP // 2
LATE_CHUNKS = [(dim, start, 4) for dim in range(3) for start in range(EARLY, QP, 4)]
LATE_CHUNKS[-1:] = [(2, QP - 4, 2), (2, QP - 2, 2)]
PIECE = 2


def flip(g):
    return g + 1 - 2 * lax.rem(g, 2)


def kernel(
    phases,
    slabs,
    v_ref,
    img_ref,
    tgt_ref,
    adj_out,
    smo_out,
    img_own,
    tgt_own,
    s_own,
    vel,
    img,
    lam,
    lam_in,
    coef,
    adj,
    des,
    des_far,
    vel_far,
    img_far,
    adj_far,
    smo,
    load_sem,
    in_send,
    in_recv,
    edge_send,
    edge_recv,
    lz_send,
    lz_recv,
    adj_send,
    adj_recv,
    d_send,
    d_recv,
    o_send,
    o_recv,
):
    phase = lax.axis_index("phase")
    slab = lax.axis_index("gz")
    q = lax.rem(phase, GROUP)
    base = phase - q
    upper_base = lax.rem(base + GROUP, phases)
    lower_base = lax.rem(base + phases - GROUP, phases)
    other = flip(slab)
    quarters = slabs * GROUP
    place = other * GROUP + q
    after = lax.rem(place + 1, quarters)
    before = lax.rem(place + quarters - 1, quarters)
    after_q, after_slab = lax.rem(after, GROUP), flip(lax.div(after, GROUP))
    before_q, before_slab = lax.rem(before, GROUP), flip(lax.div(before, GROUP))
    not_first = jnp.where(place == 0, 0.0, 1.0)
    not_last = jnp.where(place == quarters - 1, 0.0, 1.0)

    started = []

    def send(src, dst, send_sem, recv_sem, device):
        copy = pltpu.make_async_remote_copy(
            src_ref=src,
            dst_ref=dst,
            send_sem=send_sem,
            recv_sem=recv_sem,
            device_id=device,
            device_id_type=MESH,
        )
        copy.start()
        started.append(copy)

    def arrived(dst, send_sem, recv_sem):
        pltpu.make_async_remote_copy(
            src_ref=dst,
            dst_ref=dst,
            send_sem=send_sem,
            recv_sem=recv_sem,
            device_id=(phase, slab),
            device_id_type=MESH,
        ).wait_recv()

    loads = [
        pltpu.make_async_copy(img_ref.at[0], img_own, load_sem.at[0]),
        pltpu.make_async_copy(tgt_ref.at[0], tgt_own, load_sem.at[1]),
    ]
    for load in loads:
        load.start()

    partners = [(base + j, other) for j in range(GROUP)]
    partners += [(upper_base + q, slab), (lower_base + q, slab)]
    for here in (base, upper_base, lower_base):
        partners += [(here + after_q, after_slab), (here + before_q, before_slab)]
    barrier = pltpu.get_barrier_semaphore()
    for partner in partners:
        pl.semaphore_signal(barrier, inc=1, device_id=partner, device_id_type=MESH)
    pl.semaphore_wait(barrier, len(partners))

    def scatter(field, source, dest):
        for j in range(GROUP):
            send(
                source(j),
                dest,
                in_send.at[field, j],
                in_recv.at[field, q],
                (base + j, other),
            )

    def gathered(field, dest):
        for i in range(GROUP):
            arrived(dest(i), in_send.at[field, i], in_recv.at[field, i])

    inner = pl.ds(1, QP)
    early, late = pl.ds(1, EARLY), pl.ds(1 + EARLY, QP - EARLY)
    for axis in range(3):
        scatter(axis, lambda j: v_ref.at[0, axis, pl.ds(QP * j, EARLY)], vel.at[q, axis, early])
    scatter(
        5, lambda j: v_ref.at[0, 0, pl.ds(QP * j + EARLY, QP - EARLY)], vel.at[q, 0, late]
    )
    for load in loads:
        load.wait()

    @pl.loop(0, QP)
    def _(t):
        for r in range(GROUP):
            s_own[t * GROUP + r] = img_own[t * GROUP + r] - tgt_own[t * GROUP + r]

    scatter(3, lambda j: s_own.at[pl.ds(QP * j, QP)], lam.at[0, q, inner])
    scatter(
        4,
        lambda j: v_ref.at[0, pl.ds(1, 2), pl.ds(QP * j + EARLY, QP - EARLY)],
        vel.at[q, pl.ds(1, 2), late],
    )

    def scatter_image(piece):
        scatter(
            6 + piece,
            lambda j: img_ref.at[0, pl.ds(QP * j + PIECE * piece, PIECE)],
            img.at[q, pl.ds(1 + PIECE * piece, PIECE)],
        )

    def forward(number, source, dest, ways=(0, 1)):
        for way in ways:
            send(
                source,
                dest(way),
                d_send.at[way, number],
                d_recv.at[way, number],
                ((upper_base, lower_base)[way] + q, slab),
            )

    def forwarded(number, dest):
        for way in range(2):
            arrived(dest(way), d_send.at[way, number], d_recv.at[way, number])

    def send_edges(slot, buffer, dest, here):
        send(
            buffer(1),
            dest(QP + 1),
            edge_send.at[slot, 0],
            edge_recv.at[slot, 0],
            (here + before_q, before_slab),
        )
        send(
            buffer(QP),
            dest(0),
            edge_send.at[slot, 1],
            edge_recv.at[slot, 1],
            (here + after_q, after_slab),
        )

    def edges_arrived(slot, dest):
        arrived(dest(QP + 1), edge_send.at[slot, 0], edge_recv.at[slot, 0])
        arrived(dest(0), edge_send.at[slot, 1], edge_recv.at[slot, 1])

    def send_main(k):
        send(
            lam.at[k, 0, inner],
            lam_in.at[k, inner],
            lz_send.at[k],
            lz_recv.at[k],
            (lower_base + q, slab),
        )

    def lam_edges(k, i):
        if i == 0:
            return lambda plane: lam_in.at[k, plane]
        return lambda plane: lam.at[k, i, plane]

    def send_lam_edges(k, i):
        send_edges(
            GROUP * k + i,
            lambda plane: lam.at[k, i, plane],
            lam_edges(k, i),
            lower_base if i == 0 else base,
        )

    def lam_edges_arrived(k, i):
        edges_arrived(GROUP * k + i, lam_edges(k, i))

    v0_edges = lambda plane: vel.at[:, 0, plane]
    img_edges = lambda plane: img.at[:, plane]
    V_SLOT, IMG_SLOT = GROUP * STEPS, GROUP * STEPS + 1

    def forward_velocity(axis, ways):
        forward(axis, vel.at[:, axis, early], lambda way: vel_far.at[way, :, axis], ways)

    for axis in range(3):
        gathered(axis, lambda i: vel.at[i, axis, early])
        forward_velocity(axis, (0,) if axis == 2 else (0, 1))
    gathered(5, lambda i: vel.at[i, 0, late])
    send_edges(V_SLOT, v0_edges, v0_edges, base)
    gathered(3, lambda i: lam.at[0, i, inner])
    send_main(0)
    for i in range(GROUP):
        send_lam_edges(0, i)
    forward_velocity(2, (1,))
    scatter_image(0)
    scatter_image(1)
    edges_arrived(V_SLOT, v0_edges)
    gathered(4, lambda i: vel.at[i, pl.ds(1, 2), late])

    row = lax.broadcasted_iota(jnp.int32, (XW, YW), 0)
    lane = lax.broadcasted_iota(jnp.int32, (XW, YW), 1)

    def shifted(a, axis):
        size = (XW, YW)[axis]
        return pltpu.roll(a, 1, axis), pltpu.roll(a, size - 1, axis)

    dt = STEP_DT
    at_low = (row == 0, lane == 0)
    at_high = (row == XW - 1, lane == YW - 1)

    @pl.loop(0, QP)
    def _(t):
        keep_low = jnp.where(t == 0, not_first, 1.0)
        keep_high = jnp.where(t == QP - 1, not_last, 1.0)
        for i in range(GROUP):
            mid = vel[i, 0, t + 1]
            w_low = 0.5 * (vel[i, 0, t] * keep_low + mid)
            w_high = 0.5 * (vel[i, 0, t + 2] * keep_high + mid)
            total = jnp.maximum(w_high, 0.0) - jnp.minimum(w_low, 0.0)
            coef[i, t, 1] = (dt * keep_low) * jnp.maximum(w_low, 0.0)
            coef[i, t, 2] = (-dt * keep_high) * jnp.minimum(w_high, 0.0)
            for axis in range(2):
                mid = vel[i, axis + 1, t + 1]
                low, high = shifted(mid, axis)
                w_low = 0.5 * (jnp.where(at_low[axis], 0.0, low) + mid)
                w_high = 0.5 * (jnp.where(at_high[axis], 0.0, high) + mid)
                total = total + (jnp.maximum(w_high, 0.0) - jnp.minimum(w_low, 0.0))
                coef[i, t, 3 + 2 * axis] = jnp.where(
                    at_low[axis], 0.0, dt * jnp.maximum(w_low, 0.0)
                )
                coef[i, t, 4 + 2 * axis] = jnp.where(
                    at_high[axis], 0.0, -dt * jnp.minimum(w_high, 0.0)
                )
            coef[i, t, 0] = 1.0 - dt * total

    def transport(i, t, u_at, store):
        u = u_at(t + 1)
        x_low, x_high = shifted(u, 0)
        y_low, y_high = shifted(u, 1)
        near = coef[i, t, 0] * u + lam[0, i, t + 1]
        z_part = coef[i, t, 1] * u_at(t) + coef[i, t, 2] * u_at(t + 2)
        x_part = coef[i, t, 3] * x_low + coef[i, t, 4] * x_high
        y_part = coef[i, t, 5] * y_low + coef[i, t, 6] * y_high
        store(t, (near + z_part) + (x_part + y_part))

    def advance(k, i):
        def u_at(plane):
            return lam_in[k - 1, plane] if i == GROUP - 1 else lam[k - 1, i + 1, plane]

        def store(t, value):
            if k < STEPS:
                lam[k, i, t + 1] = value
            else:
                adj[i, t] = value

        if i == GROUP - 1:
            arrived(lam_in.at[k - 1, inner], lz_send.at[k - 1], lz_recv.at[k - 1])
        lam_edges_arrived(k - 1, (i + 1) % GROUP)
        for t in (0, QP - 1):
            transport(i, t, u_at, store)
        if k < STEPS:
            send_lam_edges(k, i)

        @pl.loop(0, 2)
        def _(part):
            for r in range(QP // 2 - 1):
                transport(i, 1 + part * (QP // 2 - 1) + r, u_at, store)

        if k < STEPS and i == 0:
            send_main(k)

    order = (
        [(1, 0), (1, 1), (1, 2), (1, 3), (2, 0), (2, 1), (2, 2), (3, 0), (3, 1), (2, 3)]
        + [(4, 0), (3, 2), (3, 3), (4, 1), (4, 2), (4, 3)]
    )
    pieces = QP // PIECE
    blocks = [(0, 2), (2, EARLY // PIECE + 1)]
    block_planes = [pl.ds(1, 2 * PIECE), pl.ds(1 + 2 * PIECE, EARLY - 2 * PIECE + 1)]

    def image_gathered(start, stop):
        for piece in range(start, stop):
            gathered(6 + piece, lambda i: img.at[i, pl.ds(1 + PIECE * piece, PIECE)])

    def image_far(planes):
        return lambda way: img_far.at[way, :, planes]

    for turn, (k, i) in enumerate(order):
        advance(k, i)
        if turn + 2 < pieces:
            scatter_image(turn + 2)
        if (k, i) in ((2, 0), (3, 0)):
            block = k - 2
            image_gathered(*blocks[block])
            forward(3 + block, img.at[:, block_planes[block]], image_far(block_planes[block]))
        if (k, i) == (2, 3):
            image_gathered(blocks[1][1], pieces)
            send_edges(IMG_SLOT, img_edges, img_edges, base)
        if (k, i) == (3, 3):
            edges_arrived(IMG_SLOT, img_edges)
            forward(5, img.at[:, 0], image_far(0))

    forward(6, adj.at[:, pl.ds(0, EARLY)], lambda way: adj_far.at[way])
    for i in range(GROUP):
        send(
            adj.at[i],
            adj_out.at[0, pl.ds(QP * q, QP)],
            adj_send.at[i],
            adj_recv.at[q],
            (base + i, other),
        )

    def descent(image_at, speed, state, dim, t):
        if dim == 0:
            low = image_at(t) * jnp.where(t == 0, not_first, 1.0)
            high = image_at(t + 2) * jnp.where(t == QP - 1, not_last, 1.0)
        else:
            low, high = shifted(image_at(t + 1), dim - 1)
            low = jnp.where(at_low[dim - 1], 0.0, low)
            high = jnp.where(at_high[dim - 1], 0.0, high)
        return speed - state * (0.5 * (high - low))

    def own_descent(dim, start, count):
        size = min(count, 4)

        @pl.loop(0, count // size)
        def _(step):
            for r in range(size):
                t = start + step * size + r
                for i in range(GROUP):
                    des[dim, i, t] = descent(
                        lambda plane: img[i, plane], vel[i, dim, t + 1], adj[i, t], dim, t
                    )

    def smooth(number, dim, start, count):
        @pl.loop(0, count // 2)
        def _(step):
            for r in range(2):
                t = start + step * 2 + r
                line = [des_far[0, dim, i, t] for i in range(GROUP)]
                line += [des[dim, i, t] for i in range(GROUP)]
                line += [des_far[1, dim, i, t] for i in range(GROUP)]
                for i in range(GROUP):
                    c = GROUP + i
                    value = FRAME_WEIGHTS[0] * line[c]
                    for k in range(1, TAPS + 1):
                        value = value + FRAME_WEIGHTS[k] * (line[c + k] + line[c - k])
                    smo[dim, i, t] = value

        for i in range(GROUP):
            send(
                smo.at[dim, i, pl.ds(start, count)],
                smo_out.at[0, dim, pl.ds(QP * q + start, count)],
                o_send.at[number, i],
                o_recv.at[number, q],
                (base + i, other),
            )

    early_chunks = [(dim, 0, EARLY) for dim in range(3)]
    late_chunks = LATE_CHUNKS
    chunks = early_chunks + late_chunks
    for number, (dim, start, count) in enumerate(late_chunks):
        own_descent(dim, start, count)
        part = (dim, slice(None), pl.ds(start, count))
        forward(7 + number, des.at[part], lambda way: des_far.at[(way,) + part])
    for dim in range(3):
        own_descent(dim, 0, EARLY)

    for axis in range(3):
        forwarded(axis, lambda way: vel_far.at[way, :, axis])
    for block in range(2):
        forwarded(3 + block, image_far(block_planes[block]))
    forwarded(5, image_far(0))
    forwarded(6, lambda way: adj_far.at[way])
    for number, (dim, start, count) in enumerate(early_chunks):
        for way in range(2):
            @pl.loop(0, EARLY // 4)
            def _(step):
                for r in range(4):
                    t = step * 4 + r
                    for i in range(GROUP):
                        des_far[way, dim, i, t] = descent(
                            lambda plane: img_far[way, i, plane],
                            vel_far[way, i, dim, t],
                            adj_far[way, i, t],
                            dim,
                            t,
                        )

        smooth(number, dim, start, count)
    for number, (dim, start, count) in enumerate(late_chunks):
        part = (dim, slice(None), pl.ds(start, count))
        forwarded(7 + number, lambda way: des_far.at[(way,) + part])
        smooth(len(early_chunks) + number, dim, start, count)

    for j in range(GROUP):
        arrived(adj_out.at[0, pl.ds(QP * j, QP)], adj_send.at[j], adj_recv.at[j])
    for number, (dim, start, count) in enumerate(chunks):
        for j in range(GROUP):
            arrived(
                smo_out.at[0, dim, pl.ds(QP * j + start, count)],
                o_send.at[number, j],
                o_recv.at[number, j],
            )
    for copy in started:
        copy.wait_send()


def solution(mesh):
    phases, slabs = mesh.shape["phase"], mesh.shape["gz"]

    def local(velocity, image, target):
        f32 = jnp.float32
        vmem = lambda *lead: pltpu.VMEM(lead + (XW, YW), f32)
        dma = pltpu.SemaphoreType.DMA
        planes = image.shape[1]
        late_chunks = len(LATE_CHUNKS)
        chunks = 3 + late_chunks
        fields = 6 + QP // PIECE
        anywhere = pl.BlockSpec(memory_space=pl.ANY)
        return pl.pallas_call(
            functools.partial(kernel, phases, slabs),
            out_shape=(
                jax.ShapeDtypeStruct(image.shape, f32),
                jax.ShapeDtypeStruct(velocity.shape, f32),
            ),
            in_specs=[anywhere] * 3,
            out_specs=(anywhere, anywhere),
            scratch_shapes=[
                vmem(planes),
                vmem(planes),
                vmem(planes),
                vmem(GROUP, 3, QP + 2),
                vmem(GROUP, QP + 2),
                vmem(STEPS, GROUP, QP + 2),
                vmem(STEPS, QP + 2),
                vmem(GROUP, QP, 7),
                vmem(GROUP, QP),
                vmem(3, GROUP, QP),
                vmem(2, 3, GROUP, QP),
                vmem(2, GROUP, 3, EARLY),
                vmem(2, GROUP, EARLY + 2),
                vmem(2, GROUP, EARLY),
                vmem(3, GROUP, QP),
                dma((2,)),
                dma((fields, GROUP)),
                dma((fields, GROUP)),
                dma((GROUP * STEPS + 2, 2)),
                dma((GROUP * STEPS + 2, 2)),
                dma((STEPS,)),
                dma((STEPS,)),
                dma((GROUP,)),
                dma((GROUP,)),
                dma((2, 7 + late_chunks)),
                dma((2, 7 + late_chunks)),
                dma((chunks, GROUP)),
                dma((chunks, GROUP)),
            ],
            compiler_params=pltpu.CompilerParams(
                collective_id=0,
                has_side_effects=True,
                vmem_limit_bytes=40 * 1024 * 1024,
            ),
        )(*(pltpu.with_memory_space_constraint(a, pltpu.HBM) for a in (velocity, image, target)))

    return jax.shard_map(
        local,
        mesh=mesh,
        in_specs=(
            P("phase", None, "gz", None, None),
            P("phase", "gz", None, None),
            P("phase", "gz", None, None),
        ),
        out_specs=(P("phase", "gz", None, None), P("phase", None, "gz", None, None)),
        check_vma=False,
    )
```
